32 devices in a mesh: dp: 8 (over y, x, core), vocab: 4 (over z).
Axes of the slice: x: 2, y: 2, z: 4, core: 2. Of those that a mesh axis runs over, the one named last changes fastest.
Arguments:
- hidden: bfloat16 [384, 8192], P('dp', 'vocab'), may hold values from -32 to 32
- head_weight: bfloat16 [8192, 128256], P(None, ('dp', 'vocab')), may hold values from -0.9943689 to 0.9943689
- critic_in: bfloat16 [8, 8192, 4096], P('dp', None, 'vocab'), may hold values from -0.0625 to 0.0625
- critic_out: bfloat16 [8, 4096], P('dp', 'vocab'), may hold values from -0.09375 to 0.09375
- rewards: float32 [8, 12], P('dp'), may hold values from -4 to 4
- turn_ids: int32 [8, 48], P('dp'), may hold values from 0 to 11, never falling along the last dimension, each value on 1 to 8 neighbouring positions
- owners: int32 [96, 1], P('dp'), may hold values from 0 to 7; in each aligned block of 12 rows (0 to 11, 12 to 23, ...) at most 3 rows name the same one
- actions: int32 [384], replicated, may hold values from 0 to 128255
Outputs:
- hidden_grad: float32 [384, 8192], P('dp', 'vocab')
- token_logprob: float32 [384], P('dp')
- turn_advantage: float32 [8, 12], P('dp')
The draws below stay inside these ranges and needn't reach their ends.
Inputs may be any that keep to these rules, and one draw needn't show every extreme that they name: `turn_ids`: in each row, turn numbers never fall, every number of 0 to 11 appears, and each turn has 1 to 8 tokens. `owners`: among the 12 turns of one index of dp, at most 3 name the same critic, and every critic is named by some turn.
All inputs are finite; a program needn't handle non-finite values.
Results may differ from the reference program's by a relative error of at most 0.0087.
Values may be sent and summed in bfloat16 or wider, within the bound.
A program may use at most 192 MiB of HBM per device.

```python
import math
import jax
import jax.numpy as jnp
import numpy as np
from jax import lax

D = 8192
V = 128256
CRIT_H = 4096
TOK_DEV = 48
TURN_DEV = 12
TURN_MOST = 8
CAP = 3
TOKENS = 384
TURNS = 96
N_DP = 8


def head_column(key, column):
    normal_part = jax.random.normal(jax.random.fold_in(jax.random.fold_in(key, 101), column), (D,), jnp.float32)
    normal_part = jnp.clip(normal_part, -6.0, 6.0) * (3.0 / math.sqrt(D))
    return normal_part


def draw_head_weight(key, part):
    columns = jax.vmap(lambda column: head_column(key, column))(jnp.arange(V, dtype=jnp.int32))
    return columns.T.astype(jnp.bfloat16)


def draw_hidden(key, part):
    normal_part = jnp.clip(jax.random.normal(jax.random.fold_in(key, 201), (TOKENS, D), jnp.float32), -6.0, 6.0)
    return jnp.clip(normal_part, -32.0, 32.0).astype(jnp.bfloat16)


def plant(entries, key, low, top_value):
    index_at = [jax.random.randint(jax.random.fold_in(key, axis), (), 0, length) for axis, length in enumerate(entries.shape)]
    longest = entries.shape.index(max(entries.shape))
    neighbour = index_at[:longest] + [(index_at[longest] + 1) % entries.shape[longest]] + index_at[longest + 1:]
    return entries.at[tuple(index_at)].set(low).at[tuple(neighbour)].set(top_value)


def levels(key, extent, pieces, low, largest):
    gain = 1.0
    for dim, blocks in pieces:
        steps = jax.random.uniform(jax.random.fold_in(jax.random.fold_in(key, 6), dim), (blocks,), jnp.float32, low / len(pieces), largest / len(pieces))
        gain = gain * jnp.repeat(jnp.exp(steps), extent[dim] // blocks).reshape((-1,) + (1,) * (len(extent) - 1 - dim))
    return gain


def ranked_wide(rng, dims, count, skew):
    portions = [min(1 << octave, count + 1 - (1 << octave)) * (1 << 20) // math.isqrt((1 << octave) ** skew) + 1 for octave in range((count + 1).bit_length()) if 1 << octave <= count]
    width = 1 + sum(portions) // (1 << 30)
    table = np.cumsum(np.array([max(1, weight // width) for weight in portions]))
    lot = jax.random.randint(jax.random.fold_in(rng, 1), dims, 0, int(table[len(portions) - 1]))
    start = jnp.left_shift(1, jnp.searchsorted(jnp.asarray(table, jnp.int32), lot, side="right").astype(jnp.int32))
    standing = start - 1 + jax.random.randint(jax.random.fold_in(rng, 4), dims, 0, 1 << 30) % jnp.minimum(start, count + 1 - start)
    return jax.random.permutation(jax.random.fold_in(rng, 2), count)[standing].astype(jnp.int32)


def profile(number_of, total, bound, lean):
    loads = [(1 << 20) // math.isqrt(rank ** lean) + 1 for rank in range(2, number_of + 1)]
    surplus, holding = total - bound - (number_of - 1), [1] * (number_of - 1)
    while surplus > 0:
        candidates = [i for i in range(number_of - 1) if holding[i] < bound]
        mass, remaining = sum([loads[i] for i in candidates]), surplus
        for i in candidates:
            more = min(bound - holding[i], max(1, remaining * loads[i] // mass), surplus)
            holding[i] = holding[i] + more
            surplus = surplus - more
    return np.array([bound] + holding)


def uneven(own_key, amount, total, limit, lean):
    if amount == 2:
        one = jax.random.randint(own_key, (), max(1, total - limit), min(limit, total - 1) + 1)
        return jnp.stack([one, total - one])
    tallies = jnp.asarray(profile(amount, total, limit, lean), jnp.int32)
    pairs = (amount - 1) // 2
    source_of, sink = tallies[1:1 + 2 * pairs:2], tallies[2:2 + 2 * pairs:2]
    room = jnp.minimum(source_of - 1, limit - sink)
    moved = jax.random.randint(jax.random.fold_in(own_key, 1), (pairs,), 0, 1 << 20) % (room + 1)
    tallies = tallies.at[1:1 + 2 * pairs:2].set(source_of - moved).at[2:2 + 2 * pairs:2].set(sink + moved)
    return tallies[jax.random.permutation(jax.random.fold_in(own_key, 2), amount)]


def routed_block(stream_key, own, number, rows, amount, top, reach, skew):
    order = jax.random.permutation(stream_key, amount)
    packed, ordinary = portions_of(amount, rows * top, reach, skew, True), portions_of(amount, rows * top, reach, skew, False)
    places = jnp.arange(amount)

    def named(sizes, offset_by):
        used = int((sizes > 0).sum())
        fixed = max(1, used // 4)
        passed = fixed + (places - fixed + offset_by * (used - fixed)) % max(1, amount - fixed)
        return jnp.zeros((amount,), jnp.int32).at[order[jnp.where(places < fixed, places, passed)]].set(jnp.asarray(sizes, jnp.int32))

    sizes = jnp.where(number % 4 == 0, named(packed, number // 4), named(ordinary, number - number // 4 - 1))
    mixed = jax.random.permutation(jax.random.fold_in(own, 3), amount)
    giver, sink = mixed[0:amount // 2 * 2:2], mixed[1:amount // 2 * 2:2]
    room = jnp.minimum(sizes[giver] - 1, reach - sizes[sink]) // 2
    room = jnp.where((giver == order[0]) | (sink == order[0]) | (sizes[sink] == 0), 0, jnp.maximum(room, 0))
    passed = jax.random.randint(jax.random.fold_in(own, 4), (amount // 2,), 0, 1 << 20) % (room + 1)
    sizes = sizes.at[giver].add(-passed).at[sink].add(passed)
    labels = jnp.searchsorted(jnp.cumsum(sizes), jnp.arange(rows * top), side="right").astype(jnp.int32)
    listing = labels.reshape(top, rows).T
    listing = listing[jax.random.permutation(jax.random.fold_in(own, 1), rows)]
    offset_by = jax.random.randint(jax.random.fold_in(own, 2), (rows, 1), 0, top)
    return jnp.take_along_axis(listing, (jnp.arange(top)[None, :] + offset_by) % top, axis=1)


def portions_of(count, total, bound, slope, full):
    loads = [(1 << 20) // math.isqrt(rank ** slope) + 1 for rank in range(1, count + 1)]
    largest = bound if full else min(bound, max(-(-total // count), total * loads[0] // sum(loads)))
    least = 1 if total - largest >= count - 1 else 0
    holding, surplus = [largest] + [least] * (count - 1), total - largest - least * (count - 1)
    while surplus > 0:
        movable = [i for i in range(1, count) if holding[i] < largest] or [i for i in range(1, count) if holding[i] < bound]
        mass, remaining = sum([loads[i] for i in movable]), surplus
        for i in movable:
            addition = min(bound - holding[i], max(1, remaining * loads[i] // mass), surplus)
            holding[i] = holding[i] + addition
            surplus = surplus - addition
    return np.array(holding)


def noise(key, dims, deviation, bound, pieces=(), kind=jnp.bfloat16):
    entries = deviation * jax.random.normal(key, dims, jnp.float32)
    if pieces:
        entries = entries * levels(key, dims, pieces, -0.22, 0.18)
    return jnp.clip(entries, -bound, bound).astype(kind)


def setup_inputs(seed: int = 0) -> dict:
    streams_of = jax.random.split(jax.random.key(seed), 9)
    hidden = draw_hidden(jax.random.fold_in(streams_of[8], 71), 0)
    head_weight = draw_head_weight(jax.random.fold_in(streams_of[8], 71), 0)
    critic_in = noise(streams_of[2], (N_DP, D, CRIT_H), D ** -0.5, 0.0625, ((0, 8), (2, 4)))
    critic_out = noise(streams_of[3], (N_DP, CRIT_H), CRIT_H ** -0.5, 0.09375, ((0, 8), (1, 4)))
    rewards = noise(streams_of[4], (N_DP, TURN_DEV), 1.0, 4.0, ((0, 8),), jnp.float32)
    turn_ids = jax.vmap(lambda own: jnp.searchsorted(jnp.cumsum(uneven(own, TURN_DEV, TOK_DEV, TURN_MOST, 1)), jnp.arange(TOK_DEV), side="right"))(jax.random.split(streams_of[5], N_DP)).reshape((N_DP, TOK_DEV)).astype(jnp.int32)
    owners_keys = jax.random.split(jax.random.fold_in(streams_of[6], 1), TURNS // TURN_DEV)
    owners_turns = jax.random.permutation(jax.random.fold_in(streams_of[6], 3), TURNS // TURN_DEV)
    owners = jax.vmap(lambda own, number: routed_block(jax.random.fold_in(streams_of[6], 2), own, number, TURN_DEV, N_DP, 1, CAP, 2))(owners_keys, owners_turns).reshape((TURNS, 1))
    actions = plant(ranked_wide(streams_of[7], (TOKENS,), V, 1), jax.random.fold_in(streams_of[7], 3), 0, V - 1).astype(jnp.int32)
    return {"hidden": hidden, "head_weight": head_weight, "critic_in": critic_in, "critic_out": critic_out, "rewards": rewards, "turn_ids": turn_ids, "owners": owners, "actions": actions}


epsilon = 1e-05
loss_scale = 32.0

def rms_norm(values):
    return values * lax.rsqrt(lax.optimization_barrier(jnp.mean(values * values, axis=-1, keepdims=True)) + epsilon)

def reference(hidden, head_weight, critic_in, critic_out, rewards, turn_ids, owners, actions):
    position = jnp.arange(TOK_DEV, dtype=jnp.int32)
    turn_range = jnp.arange(TURN_DEV, dtype=jnp.int32)
    member = turn_ids[:, None, :] == turn_range[None, :, None]
    last_pos = lax.optimization_barrier(jnp.max(jnp.where(member, position[None, None, :], -1), axis=2))
    end_pick = (position[None, None, :] == last_pos[:, :, None]).astype(jnp.float32)
    shard_hidden = hidden.astype(jnp.float32).reshape(N_DP, TOK_DEV, D)
    end_rows = jnp.einsum('pti,pid->ptd', end_pick, shard_hidden, precision=lax.Precision.HIGHEST)
    end_rows = end_rows.reshape(TURNS, D)
    owner_of = owners[:, 0].astype(jnp.int32)

    def score(item):
        row_values, index = item
        normed = rms_norm(row_values[None, :]).astype(jnp.bfloat16)
        inner = jnp.dot(normed, critic_in[index], preferred_element_type=jnp.float32)
        active = jax.nn.silu(inner).astype(jnp.bfloat16)
        return jnp.dot(active, critic_out[index][:, None], preferred_element_type=jnp.float32)[0, 0]
    turn_value = lax.map(score, (end_rows, owner_of))
    advantage = rewards - turn_value.reshape(N_DP, TURN_DEV)
    token_adv = lax.optimization_barrier(jnp.sum(jnp.where(member, advantage[:, :, None], 0.0), axis=1)).reshape(TOKENS)
    logits = jnp.dot(hidden, head_weight, preferred_element_type=jnp.float32)
    row_top = lax.optimization_barrier(jnp.max(logits, axis=1))
    shifted = jnp.exp(logits - row_top[:, None])
    row_mass = lax.optimization_barrier(jnp.sum(shifted, axis=1))
    vocab_range = jnp.arange(V, dtype=jnp.int32)
    hit = vocab_range[None, :] == actions[:, None]
    picked = lax.optimization_barrier(jnp.sum(jnp.where(hit, logits, 0.0), axis=1))
    logprob = picked - row_top - jnp.log(row_mass)
    grad_logits = (loss_scale * token_adv[:, None] * (shifted / row_mass[:, None] - hit.astype(jnp.float32))).astype(jnp.bfloat16)
    hidden_grad = lax.dot_general(grad_logits, head_weight, (((1,), (1,)), ((), ())), preferred_element_type=jnp.float32)
    return (hidden_grad, logprob, advantage)
```

```python
import functools

import jax
import jax.numpy as jnp
from jax import lax
from jax.experimental import pallas as pl
from jax.experimental.pallas import tpu as pltpu
from jax.sharding import PartitionSpec as P


epsilon = 1e-05
loss_scale = 32.0
MESH = pl.DeviceIdType.MESH


def rms_norm(values):
    return values * lax.rsqrt(jnp.mean(values * values, axis=-1, keepdims=True) + epsilon)


def exchange_kernel(ranks_dp, ranks_vocab, over_vocab, block_ref, all_ref, send_sem, recv_sem, own_sem):
    my_dp, my_vocab = lax.axis_index("dp"), lax.axis_index("vocab")
    count = ranks_dp * ranks_vocab if over_vocab else ranks_dp
    me = my_dp * ranks_vocab + my_vocab if over_vocab else my_dp

    def place(step):
        peer = lax.rem(me + step, count)
        if over_vocab:
            return (lax.div(peer, ranks_vocab), lax.rem(peer, ranks_vocab))
        return (peer, my_vocab)

    barrier = pltpu.get_barrier_semaphore()
    for step in range(1, count):
        pl.semaphore_signal(barrier, inc=1, device_id=place(step), device_id_type=MESH)
    pl.semaphore_wait(barrier, count - 1)
    own = pltpu.make_async_copy(block_ref, all_ref.at[me], own_sem)
    own.start()
    copies = []
    for step in range(1, count):
        copy = pltpu.make_async_remote_copy(
            src_ref=block_ref,
            dst_ref=all_ref.at[me],
            send_sem=send_sem.at[step],
            recv_sem=recv_sem.at[step],
            device_id=place(step),
            device_id_type=MESH,
        )
        copy.start()
        copies.append(copy)
    own.wait()
    for copy in copies:
        copy.wait()


def exchange(block, over_vocab, collective_id):
    ranks_dp, ranks_vocab = lax.axis_size("dp"), lax.axis_size("vocab")
    count = ranks_dp * ranks_vocab if over_vocab else ranks_dp
    return pl.pallas_call(
        functools.partial(exchange_kernel, ranks_dp, ranks_vocab, over_vocab),
        out_shape=jax.ShapeDtypeStruct((count,) + block.shape, block.dtype),
        in_specs=[pl.BlockSpec(memory_space=pltpu.VMEM)],
        out_specs=pl.BlockSpec(memory_space=pltpu.VMEM),
        scratch_shapes=[
            pltpu.SemaphoreType.DMA((count,)),
            pltpu.SemaphoreType.DMA((count,)),
            pltpu.SemaphoreType.DMA,
        ],
        compiler_params=pltpu.CompilerParams(collective_id=collective_id, has_side_effects=True),
    )(block)


def halve(parts, axis_name, bit, axis):
    ranks = lax.axis_size(axis_name)
    mine = (lax.axis_index(axis_name) >> bit) & 1
    first, second = [lax.index_in_dim(parts, i, axis, keepdims=False) for i in (0, 1)]
    kept = jnp.where(mine == 0, first, second)
    sent = jnp.where(mine == 0, second, first)
    got = lax.ppermute(sent, axis_name, [(i, i ^ (1 << bit)) for i in range(ranks)])
    return kept.astype(jnp.float32) + got.astype(jnp.float32)


def advance(chunks, number, orders, step):
    states, order = chunks[number], orders[number % 2]
    if len(states) == step + 1:
        axis = sorted(order[step:], reverse=True).index(order[step])
        states.append(halve(states[-1], "dp", order[step], axis).astype(jnp.bfloat16))
    return states[step + 1]


def on_device(hidden, head_weight, critic_in, critic_out, rewards, turn_ids, owners, actions):
    ranks_dp = lax.axis_size("dp")
    ranks_vocab = lax.axis_size("vocab")
    my_dp, my_vocab = lax.axis_index("dp"), lax.axis_index("vocab")
    tok_dev = hidden.shape[0]
    tokens = tok_dev * ranks_dp
    width = hidden.shape[1]
    turn_dev = rewards.shape[1]
    turns = turn_dev * ranks_dp
    slot_count = max(2, 2 * turn_dev // ranks_dp)
    vocab_local = head_weight.shape[1]

    lanes = -(-max(tok_dev, turn_dev) // 128) * 128

    def row(values):
        return jnp.pad(values.astype(jnp.float32), (0, lanes - values.shape[0]))[None, :]

    facts = jnp.concatenate(
        [row(turn_ids[0]), row(owners[:, 0]), row(rewards[0]), jnp.zeros((5, lanes), jnp.float32)]
    )
    facts = exchange(facts, False, 1)
    ids_all = facts[:, 0, :tok_dev].astype(jnp.int32)
    owner_all = facts[:, 1, :turn_dev].astype(jnp.int32)
    rewards_all = facts[:, 2, :turn_dev]

    feats = lax.all_gather(hidden, "vocab", axis=1, tiled=True)
    hidden_all = lax.all_gather(feats, "dp", axis=0, tiled=True)

    position = jnp.arange(tok_dev, dtype=jnp.int32)
    turn_range = jnp.arange(turn_dev, dtype=jnp.int32)
    member = ids_all[:, None, :] == turn_range[None, :, None]
    last_pos = jnp.max(jnp.where(member, position, -1), axis=2)
    earlier = (owner_all[:, None, :] == owner_all[:, :, None]) & (
        turn_range[None, :] < turn_range[:, None]
    )
    slot_of = jnp.sum(earlier.astype(jnp.int32), axis=2)
    per_critic = ranks_dp * slot_count
    place = (owner_all * ranks_dp + jnp.arange(ranks_dp, dtype=jnp.int32)[:, None]) * slot_count
    place = (place + slot_of).reshape(turns)
    end_token = (jnp.arange(ranks_dp, dtype=jnp.int32)[:, None] * tok_dev + last_pos).reshape(turns)
    slots = my_dp * per_critic + jnp.arange(per_critic, dtype=jnp.int32)
    token_of_slot = jnp.sum(
        jnp.where(place[None, :] == slots[:, None], end_token[None, :] + 1, 0), axis=1
    ) - 1
    pick = (jnp.arange(tokens, dtype=jnp.int32)[None, :] == token_of_slot[:, None]).astype(
        jnp.bfloat16
    )
    place_tok = jnp.sum(
        jnp.where(member, place.reshape(ranks_dp, turn_dev)[:, :, None], 0), axis=1
    ).reshape(tokens)
    reward_tok = jnp.sum(jnp.where(member, rewards_all[:, :, None], 0.0), axis=1).reshape(tokens)
    place_own = lax.dynamic_slice_in_dim(place, my_dp * turn_dev, turn_dev, 0)

    rows = jnp.dot(pick, hidden_all, preferred_element_type=jnp.float32)
    normed = rms_norm(rows).astype(jnp.bfloat16)
    inner = jnp.dot(normed, critic_in[0], preferred_element_type=jnp.float32)
    active = jax.nn.silu(inner).astype(jnp.bfloat16)
    value_part = jnp.sum(
        active.astype(jnp.float32) * critic_out[0].astype(jnp.float32)[None, :], axis=1
    )

    logits = jnp.dot(hidden_all, head_weight, preferred_element_type=jnp.float32)
    first_col = (my_dp * ranks_vocab + my_vocab) * vocab_local
    hit = jnp.arange(vocab_local, dtype=jnp.int32)[None, :] == (actions - first_col)[:, None]
    picked_part = jnp.sum(jnp.where(hit, logits, 0.0), axis=1)
    top_part = jnp.max(logits, axis=1)
    mass_part = jnp.sum(jnp.exp(logits - top_part[:, None]), axis=1)

    stats = jnp.stack(
        [top_part, mass_part, picked_part, jnp.pad(value_part, (0, tokens - per_critic))]
        + [jnp.zeros((tokens,), jnp.float32)] * 4
    )
    stats = exchange(stats, True, 2)
    row_top = jnp.max(stats[:, 0], axis=0)
    row_mass = jnp.sum(stats[:, 1] * jnp.exp(stats[:, 0] - row_top[None, :]), axis=0)
    picked = jnp.sum(stats[:, 2], axis=0)
    logprob_all = picked - row_top - jnp.log(row_mass)
    token_logprob = lax.dynamic_slice_in_dim(logprob_all, my_dp * tok_dev, tok_dev, 0)
    values = jnp.sum(
        stats[:, 3, :per_critic].reshape(ranks_dp, ranks_vocab, per_critic), axis=1
    ).reshape(-1)
    all_places = jnp.arange(ranks_dp * per_critic, dtype=jnp.int32)

    def value_at(places):
        return jnp.sum(jnp.where(places[:, None] == all_places[None, :], values[None, :], 0.0), axis=1)

    advantage = rewards[0] - value_at(place_own)
    token_adv = reward_tok - value_at(place_tok)

    probs = jnp.exp(logits - row_top[:, None]) / row_mass[:, None]
    grad_logits = (loss_scale * token_adv[:, None] * (probs - hit.astype(jnp.float32))).astype(
        jnp.bfloat16
    )
    grad_logits = lax.optimization_barrier(grad_logits)

    dp_bits = list(range(ranks_dp.bit_length() - 1))
    orders = (dp_bits, dp_bits[:1] + dp_bits[:0:-1])
    half = width // 2
    chunks = []
    for number in range(2 * ranks_vocab):
        ready = []
        for back in range(len(dp_bits)):
            if number - 2 - back >= 0:
                ready.append(advance(chunks, number - 2 - back, orders, back))
        if ready:
            grad_logits = lax.optimization_barrier((grad_logits, *ready))[0]
        weight = lax.slice_in_dim(head_weight, number * half, (number + 1) * half, axis=0)
        part = lax.dot_general(
            grad_logits, weight, (((1,), (1,)), ((), ())), preferred_element_type=jnp.float32
        ).astype(jnp.bfloat16)
        chunks.append([part.reshape((2,) * len(dp_bits) + (tok_dev, half))])
    for step in range(len(dp_bits)):
        for number in range(2 * ranks_vocab):
            advance(chunks, number, orders, step)
    blocks = [[chunks[2 * i + k][-1] for k in (0, 1)] for i in range(ranks_vocab)]
    bit = 0
    while len(blocks) > 1:
        blocks = [
            [
                halve(jnp.stack([blocks[i][k], blocks[i + 1][k]]), "vocab", bit, 0)
                for k in (0, 1)
            ]
            for i in range(0, len(blocks), 2)
        ]
        if len(blocks) > 1:
            blocks = [[x.astype(jnp.bfloat16) for x in pair] for pair in blocks]
        bit += 1
    hidden_grad = jnp.concatenate(blocks[0], axis=1)
    return (hidden_grad, token_logprob, advantage[None, :])


def solution(mesh):
    return jax.shard_map(
        on_device,
        mesh=mesh,
        in_specs=(
            P("dp", "vocab"),
            P(None, ("dp", "vocab")),
            P("dp", None, "vocab"),
            P("dp", "vocab"),
            P("dp", None),
            P("dp", None),
            P("dp", None),
            P(),
        ),
        out_specs=(P("dp", "vocab"), P("dp"), P("dp", None)),
        check_vma=False,
    )
```

```python
import functools

import jax
import jax.numpy as jnp
from jax import lax
from jax.experimental import pallas as pl
from jax.experimental.pallas import tpu as pltpu
from jax.sharding import PartitionSpec as P


epsilon = 1e-05
loss_scale = 32.0
MESH = pl.DeviceIdType.MESH


def rms_norm(values):
    return values * lax.rsqrt(jnp.mean(values * values, axis=-1, keepdims=True) + epsilon)


def exchange_kernel(ranks_dp, ranks_vocab, over_vocab, block_ref, all_ref, send_sem, recv_sem, own_sem):
    my_dp, my_vocab = lax.axis_index("dp"), lax.axis_index("vocab")
    count = ranks_dp * ranks_vocab if over_vocab else ranks_dp
    me = my_dp * ranks_vocab + my_vocab if over_vocab else my_dp

    def place(step):
        peer = lax.rem(me + step, count)
        if over_vocab:
            return (lax.div(peer, ranks_vocab), lax.rem(peer, ranks_vocab))
        return (peer, my_vocab)

    barrier = pltpu.get_barrier_semaphore()
    for step in range(1, count):
        pl.semaphore_signal(barrier, inc=1, device_id=place(step), device_id_type=MESH)
    pl.semaphore_wait(barrier, count - 1)
    own = pltpu.make_async_copy(block_ref, all_ref.at[me], own_sem)
    own.start()
    copies = []
    for step in range(1, count):
        copy = pltpu.make_async_remote_copy(
            src_ref=block_ref,
            dst_ref=all_ref.at[me],
            send_sem=send_sem.at[step],
            recv_sem=recv_sem.at[step],
            device_id=place(step),
            device_id_type=MESH,
        )
        copy.start()
        copies.append(copy)
    own.wait()
    for copy in copies:
        copy.wait()


def exchange(block, over_vocab, collective_id):
    ranks_dp, ranks_vocab = lax.axis_size("dp"), lax.axis_size("vocab")
    count = ranks_dp * ranks_vocab if over_vocab else ranks_dp
    return pl.pallas_call(
        functools.partial(exchange_kernel, ranks_dp, ranks_vocab, over_vocab),
        out_shape=jax.ShapeDtypeStruct((count,) + block.shape, block.dtype),
        in_specs=[pl.BlockSpec(memory_space=pltpu.VMEM)],
        out_specs=pl.BlockSpec(memory_space=pltpu.VMEM),
        scratch_shapes=[
            pltpu.SemaphoreType.DMA((count,)),
            pltpu.SemaphoreType.DMA((count,)),
            pltpu.SemaphoreType.DMA,
        ],
        compiler_params=pltpu.CompilerParams(collective_id=collective_id, has_side_effects=True),
    )(block)


def gather_kernel(
    ranks_dp, ranks_vocab, x_ref, facts_ref, all_ref, facts_all_ref,
    own_sem, facts_send, facts_recv, side_send, side_recv, send_sem, recv_sem,
):
    me, col = lax.axis_index("dp"), lax.axis_index("vocab")
    width = x_ref.shape[1]
    half = width // 2
    bits = list(range(1, ranks_dp.bit_length() - 1))
    orders = (bits + [0], bits[::-1] + [0])
    rounds = len(orders[0])

    barrier = pltpu.get_barrier_semaphore()
    for step in range(1, ranks_dp):
        pl.semaphore_signal(barrier, inc=1, device_id=(me ^ step, col), device_id_type=MESH)
    for step in range(1, ranks_vocab):
        pl.semaphore_signal(barrier, inc=1, device_id=(me, col ^ step), device_id_type=MESH)
    pl.semaphore_wait(barrier, ranks_dp + ranks_vocab - 2)

    mine = all_ref.at[me, :, pl.ds(pl.multiple_of(col * width, 128), width)]
    own = [
        pltpu.make_async_copy(x_ref, mine, own_sem.at[0]),
        pltpu.make_async_copy(facts_ref, facts_all_ref.at[me], own_sem.at[1]),
    ]
    for copy in own:
        copy.start()
    side = {}
    for step in range(1, ranks_vocab):
        side[step] = pltpu.make_async_remote_copy(
            src_ref=x_ref, dst_ref=mine,
            send_sem=side_send.at[step], recv_sem=side_recv.at[step],
            device_id=(me, col ^ step), device_id_type=MESH,
        )
        side[step].start()
    others = []
    for step in range(1, ranks_dp):
        copy = pltpu.make_async_remote_copy(
            src_ref=facts_ref, dst_ref=facts_all_ref.at[me],
            send_sem=facts_send.at[step], recv_sem=facts_recv.at[step],
            device_id=(me ^ step, col), device_id_type=MESH,
        )
        copy.start()
        others.append(copy)
    for copy in own:
        copy.wait()

    moves = {}
    for time in range(ranks_vocab + rounds - 1):
        for turn in range(rounds - 1, -1, -1):
            piece = time - turn
            if not 0 <= piece < ranks_vocab:
                continue
            if turn == 0 and piece > 0:
                side[piece].wait_recv()
            for part in (0, 1):
                order = orders[part]
                if turn > 0:
                    for copy in moves[piece, part, turn - 1]:
                        copy.wait_recv()
                start = pl.multiple_of((col ^ piece) * width + part * half, 128)
                started = []
                for k in range(1 << turn):
                    mask = sum(1 << order[i] for i in range(turn) if k >> i & 1)
                    block = all_ref.at[me ^ mask, :, pl.ds(start, half)]
                    slot = (1 << turn) + k
                    copy = pltpu.make_async_remote_copy(
                        src_ref=block, dst_ref=block,
                        send_sem=send_sem.at[piece, part, slot],
                        recv_sem=recv_sem.at[piece, part, slot],
                        device_id=(me ^ (1 << order[turn]), col), device_id_type=MESH,
                    )
                    copy.start()
                    started.append(copy)
                moves[piece, part, turn] = started
    for (piece, part, turn), started in moves.items():
        for copy in started:
            if turn == rounds - 1:
                copy.wait_recv()
            copy.wait_send()
    for copy in side.values():
        copy.wait_send()
    for copy in others:
        copy.wait()


def gather(x, facts):
    ranks_dp, ranks_vocab = lax.axis_size("dp"), lax.axis_size("vocab")
    dma = pltpu.SemaphoreType.DMA
    everything, facts_all = pl.pallas_call(
        functools.partial(gather_kernel, ranks_dp, ranks_vocab),
        out_shape=(
            jax.ShapeDtypeStruct((ranks_dp, x.shape[0], x.shape[1] * ranks_vocab), x.dtype),
            jax.ShapeDtypeStruct((ranks_dp,) + facts.shape, facts.dtype),
        ),
        in_specs=[pl.BlockSpec(memory_space=pltpu.VMEM)] * 2,
        out_specs=[pl.BlockSpec(memory_space=pltpu.VMEM)] * 2,
        scratch_shapes=[
            dma((2,)),
            dma((ranks_dp,)),
            dma((ranks_dp,)),
            dma((ranks_vocab,)),
            dma((ranks_vocab,)),
            dma((ranks_vocab, 2, ranks_dp)),
            dma((ranks_vocab, 2, ranks_dp)),
        ],
        compiler_params=pltpu.CompilerParams(collective_id=1, has_side_effects=True),
    )(x, facts)
    return everything.reshape(-1, everything.shape[2]), facts_all


def halve(parts, axis_name, bit, axis):
    ranks = lax.axis_size(axis_name)
    mine = (lax.axis_index(axis_name) >> bit) & 1
    first, second = [lax.index_in_dim(parts, i, axis, keepdims=False) for i in (0, 1)]
    kept = jnp.where(mine == 0, first, second)
    sent = jnp.where(mine == 0, second, first)
    got = lax.ppermute(sent, axis_name, [(i, i ^ (1 << bit)) for i in range(ranks)])
    return kept.astype(jnp.float32) + got.astype(jnp.float32)


def advance(chunks, number, orders, step):
    states, order = chunks[number], orders[number % 2]
    if len(states) == step + 1:
        axis = sorted(order[step:], reverse=True).index(order[step])
        states.append(halve(states[-1], "dp", order[step], axis).astype(jnp.bfloat16))
    return states[step + 1]


def on_device(hidden, head_weight, critic_in, critic_out, rewards, turn_ids, owners, actions):
    ranks_dp = lax.axis_size("dp")
    ranks_vocab = lax.axis_size("vocab")
    my_dp, my_vocab = lax.axis_index("dp"), lax.axis_index("vocab")
    tok_dev = hidden.shape[0]
    tokens = tok_dev * ranks_dp
    width = hidden.shape[1]
    turn_dev = rewards.shape[1]
    turns = turn_dev * ranks_dp
    slot_count = max(2, 2 * turn_dev // ranks_dp)
    vocab_local = head_weight.shape[1]

    lanes = -(-max(tok_dev, turn_dev) // 128) * 128

    def row(values):
        return jnp.pad(values.astype(jnp.float32), (0, lanes - values.shape[0]))[None, :]

    facts = jnp.concatenate(
        [row(turn_ids[0]), row(owners[:, 0]), row(rewards[0]), jnp.zeros((5, lanes), jnp.float32)]
    )
    hidden_all, facts = gather(hidden, facts)
    ids_all = facts[:, 0, :tok_dev].astype(jnp.int32)
    owner_all = facts[:, 1, :turn_dev].astype(jnp.int32)
    rewards_all = facts[:, 2, :turn_dev]

    position = jnp.arange(tok_dev, dtype=jnp.int32)
    turn_range = jnp.arange(turn_dev, dtype=jnp.int32)
    member = ids_all[:, None, :] == turn_range[None, :, None]
    last_pos = jnp.max(jnp.where(member, position, -1), axis=2)
    earlier = (owner_all[:, None, :] == owner_all[:, :, None]) & (
        turn_range[None, :] < turn_range[:, None]
    )
    slot_of = jnp.sum(earlier.astype(jnp.int32), axis=2)
    per_critic = ranks_dp * slot_count
    place = (owner_all * ranks_dp + jnp.arange(ranks_dp, dtype=jnp.int32)[:, None]) * slot_count
    place = (place + slot_of).reshape(turns)
    end_token = (jnp.arange(ranks_dp, dtype=jnp.int32)[:, None] * tok_dev + last_pos).reshape(turns)
    slots = my_dp * per_critic + jnp.arange(per_critic, dtype=jnp.int32)
    token_of_slot = jnp.sum(
        jnp.where(place[None, :] == slots[:, None], end_token[None, :] + 1, 0), axis=1
    ) - 1
    pick = (jnp.arange(tokens, dtype=jnp.int32)[None, :] == token_of_slot[:, None]).astype(
        jnp.bfloat16
    )
    place_tok = jnp.sum(
        jnp.where(member, place.reshape(ranks_dp, turn_dev)[:, :, None], 0), axis=1
    ).reshape(tokens)
    reward_tok = jnp.sum(jnp.where(member, rewards_all[:, :, None], 0.0), axis=1).reshape(tokens)
    place_own = lax.dynamic_slice_in_dim(place, my_dp * turn_dev, turn_dev, 0)

    rows = jnp.dot(pick, hidden_all, preferred_element_type=jnp.float32)
    normed = rms_norm(rows).astype(jnp.bfloat16)
    inner = jnp.dot(normed, critic_in[0], preferred_element_type=jnp.float32)
    active = jax.nn.silu(inner).astype(jnp.bfloat16)
    value_part = jnp.sum(
        active.astype(jnp.float32) * critic_out[0].astype(jnp.float32)[None, :], axis=1
    )

    logits = jnp.dot(hidden_all, head_weight, preferred_element_type=jnp.float32)
    first_col = (my_dp * ranks_vocab + my_vocab) * vocab_local
    hit = jnp.arange(vocab_local, dtype=jnp.int32)[None, :] == (actions - first_col)[:, None]
    picked_part = jnp.sum(jnp.where(hit, logits, 0.0), axis=1)
    top_part = jnp.max(logits, axis=1)
    mass_part = jnp.sum(jnp.exp(logits - top_part[:, None]), axis=1)

    stats = jnp.stack(
        [top_part, mass_part, picked_part, jnp.pad(value_part, (0, tokens - per_critic))]
        + [jnp.zeros((tokens,), jnp.float32)] * 4
    )
    stats = exchange(stats, True, 2)
    row_top = jnp.max(stats[:, 0], axis=0)
    row_mass = jnp.sum(stats[:, 1] * jnp.exp(stats[:, 0] - row_top[None, :]), axis=0)
    picked = jnp.sum(stats[:, 2], axis=0)
    logprob_all = picked - row_top - jnp.log(row_mass)
    token_logprob = lax.dynamic_slice_in_dim(logprob_all, my_dp * tok_dev, tok_dev, 0)
    values = jnp.sum(
        stats[:, 3, :per_critic].reshape(ranks_dp, ranks_vocab, per_critic), axis=1
    ).reshape(-1)
    all_places = jnp.arange(ranks_dp * per_critic, dtype=jnp.int32)

    def value_at(places):
        return jnp.sum(jnp.where(places[:, None] == all_places[None, :], values[None, :], 0.0), axis=1)

    advantage = rewards[0] - value_at(place_own)
    token_adv = reward_tok - value_at(place_tok)

    probs = jnp.exp(logits - row_top[:, None]) / row_mass[:, None]
    grad_logits = (loss_scale * token_adv[:, None] * (probs - hit.astype(jnp.float32))).astype(
        jnp.bfloat16
    )
    grad_logits = lax.optimization_barrier(grad_logits)

    dp_bits = list(range(ranks_dp.bit_length() - 1))
    orders = (dp_bits, dp_bits[:1] + dp_bits[:0:-1])
    half = width // 2
    chunks = []
    for number in range(2 * ranks_vocab):
        weight = lax.slice_in_dim(head_weight, number * half, (number + 1) * half, axis=0)
        part = lax.dot_general(
            grad_logits, weight, (((1,), (1,)), ((), ())), preferred_element_type=jnp.float32
        ).astype(jnp.bfloat16)
        chunks.append([part.reshape((2,) * len(dp_bits) + (tok_dev, half))])
    for step in range(len(dp_bits)):
        for number in range(2 * ranks_vocab):
            advance(chunks, number, orders, step)
    blocks = [[chunks[2 * i + k][-1] for k in (0, 1)] for i in range(ranks_vocab)]
    bit = 0
    while len(blocks) > 1:
        joined = []
        for i in range(0, len(blocks), 2):
            pair = []
            for k in (0, 1):
                both = jnp.stack([blocks[i][k], blocks[i + 1][k]])
                pair.append(halve(both, "vocab", bit, 0))
            joined.append(pair)
        blocks = joined
        if len(blocks) > 1:
            blocks = [[x.astype(jnp.bfloat16) for x in pair] for pair in blocks]
        bit += 1
    hidden_grad = jnp.concatenate(blocks[0], axis=1)
    return (hidden_grad, token_logprob, advantage[None, :])


def solution(mesh):
    return jax.shard_map(
        on_device,
        mesh=mesh,
        in_specs=(
            P("dp", "vocab"),
            P(None, ("dp", "vocab")),
            P("dp", None, "vocab"),
            P("dp", "vocab"),
            P("dp", None),
            P("dp", None),
            P("dp", None),
            P(),
        ),
        out_specs=(P("dp", "vocab"), P("dp"), P("dp", None)),
        check_vma=False,
    )
```

```python
import functools

import jax
import jax.numpy as jnp
from jax import lax
from jax.experimental import pallas as pl
from jax.experimental.pallas import tpu as pltpu
from jax.sharding import PartitionSpec as P


epsilon = 1e-05
loss_scale = 32.0
MESH = pl.DeviceIdType.MESH


def rms_norm(values):
    return values * lax.rsqrt(jnp.mean(values * values, axis=-1, keepdims=True) + epsilon)


def exchange_kernel(ranks_dp, ranks_vocab, block_ref, all_ref, send_sem, recv_sem, own_sem):
    me, col = lax.axis_index("dp"), lax.axis_index("vocab")
    across = [(me, col ^ step) for step in range(1, ranks_vocab)]
    along = [(me ^ step, col) for step in range(1, ranks_dp)]
    barrier = pltpu.get_barrier_semaphore()
    for peer in across + along:
        pl.semaphore_signal(barrier, inc=1, device_id=peer, device_id_type=MESH)
    pl.semaphore_wait(barrier, ranks_dp + ranks_vocab - 2)
    own = pltpu.make_async_copy(block_ref, all_ref.at[me, col], own_sem)
    own.start()

    def send(source, target, peers, first):
        copies = []
        for number, peer in enumerate(peers):
            copy = pltpu.make_async_remote_copy(
                src_ref=source,
                dst_ref=target,
                send_sem=send_sem.at[first + number],
                recv_sem=recv_sem.at[first + number],
                device_id=peer,
                device_id_type=MESH,
            )
            copy.start()
            copies.append(copy)
        return copies

    for copy in send(block_ref, all_ref.at[me, col], across, 0):
        copy.wait()
    own.wait()
    for copy in send(all_ref.at[me], all_ref.at[me], along, len(across)):
        copy.wait()


def exchange(block, collective_id):
    ranks_dp, ranks_vocab = lax.axis_size("dp"), lax.axis_size("vocab")
    copies = ranks_dp + ranks_vocab - 2
    everything = pl.pallas_call(
        functools.partial(exchange_kernel, ranks_dp, ranks_vocab),
        out_shape=jax.ShapeDtypeStruct((ranks_dp, ranks_vocab) + block.shape, block.dtype),
        in_specs=[pl.BlockSpec(memory_space=pltpu.VMEM)],
        out_specs=pl.BlockSpec(memory_space=pltpu.VMEM),
        scratch_shapes=[
            pltpu.SemaphoreType.DMA((copies,)),
            pltpu.SemaphoreType.DMA((copies,)),
            pltpu.SemaphoreType.DMA,
        ],
        compiler_params=pltpu.CompilerParams(collective_id=collective_id, has_side_effects=True),
    )(block)
    return everything.reshape((-1,) + block.shape)


def gather_kernel(
    ranks_dp, ranks_vocab, x_ref, facts_ref, all_ref, facts_all_ref,
    own_sem, facts_send, facts_recv, side_send, side_recv, send_sem, recv_sem,
):
    me, col = lax.axis_index("dp"), lax.axis_index("vocab")
    width = x_ref.shape[1]
    half = width // 2
    bits = list(range(1, ranks_dp.bit_length() - 1))
    orders = (bits + [0], bits[::-1] + [0])
    rounds = len(orders[0])

    barrier = pltpu.get_barrier_semaphore()
    for step in range(1, ranks_dp):
        pl.semaphore_signal(barrier, inc=1, device_id=(me ^ step, col), device_id_type=MESH)
    for step in range(1, ranks_vocab):
        pl.semaphore_signal(barrier, inc=1, device_id=(me, col ^ step), device_id_type=MESH)
    pl.semaphore_wait(barrier, ranks_dp + ranks_vocab - 2)

    mine = all_ref.at[me, :, pl.ds(pl.multiple_of(col * width, 128), width)]
    own = [
        pltpu.make_async_copy(x_ref, mine, own_sem.at[0]),
        pltpu.make_async_copy(facts_ref, facts_all_ref.at[me], own_sem.at[1]),
    ]
    for copy in own:
        copy.start()
    side = {}
    for step in range(1, ranks_vocab):
        side[step] = pltpu.make_async_remote_copy(
            src_ref=x_ref, dst_ref=mine,
            send_sem=side_send.at[step], recv_sem=side_recv.at[step],
            device_id=(me, col ^ step), device_id_type=MESH,
        )
        side[step].start()
    others = []
    for step in range(1, ranks_dp):
        copy = pltpu.make_async_remote_copy(
            src_ref=facts_ref, dst_ref=facts_all_ref.at[me],
            send_sem=facts_send.at[step], recv_sem=facts_recv.at[step],
            device_id=(me ^ step, col), device_id_type=MESH,
        )
        copy.start()
        others.append(copy)
    for copy in own:
        copy.wait()

    moves = {}
    for time in range(ranks_vocab + rounds - 1):
        for turn in range(rounds - 1, -1, -1):
            piece = time - turn
            if not 0 <= piece < ranks_vocab:
                continue
            if turn == 0 and piece > 0:
                side[piece].wait_recv()
            for part in (0, 1):
                order = orders[part]
                if turn > 0:
                    for copy in moves[piece, part, turn - 1]:
                        copy.wait_recv()
                start = pl.multiple_of((col ^ piece) * width + part * half, 128)
                started = []
                for k in range(1 << turn):
                    mask = sum(1 << order[i] for i in range(turn) if k >> i & 1)
                    block = all_ref.at[me ^ mask, :, pl.ds(start, half)]
                    slot = (1 << turn) + k
                    copy = pltpu.make_async_remote_copy(
                        src_ref=block, dst_ref=block,
                        send_sem=send_sem.at[piece, part, slot],
                        recv_sem=recv_sem.at[piece, part, slot],
                        device_id=(me ^ (1 << order[turn]), col), device_id_type=MESH,
                    )
                    copy.start()
                    started.append(copy)
                moves[piece, part, turn] = started
    for (piece, part, turn), started in moves.items():
        for copy in started:
            if turn == rounds - 1:
                copy.wait_recv()
            copy.wait_send()
    for copy in side.values():
        copy.wait_send()
    for copy in others:
        copy.wait()


def gather(x, facts):
    ranks_dp, ranks_vocab = lax.axis_size("dp"), lax.axis_size("vocab")
    dma = pltpu.SemaphoreType.DMA
    everything, facts_all = pl.pallas_call(
        functools.partial(gather_kernel, ranks_dp, ranks_vocab),
        out_shape=(
            jax.ShapeDtypeStruct((ranks_dp, x.shape[0], x.shape[1] * ranks_vocab), x.dtype),
            jax.ShapeDtypeStruct((ranks_dp,) + facts.shape, facts.dtype),
        ),
        in_specs=[pl.BlockSpec(memory_space=pltpu.VMEM)] * 2,
        out_specs=[pl.BlockSpec(memory_space=pltpu.VMEM)] * 2,
        scratch_shapes=[
            dma((2,)),
            dma((ranks_dp,)),
            dma((ranks_dp,)),
            dma((ranks_vocab,)),
            dma((ranks_vocab,)),
            dma((ranks_vocab, 2, ranks_dp)),
            dma((ranks_vocab, 2, ranks_dp)),
        ],
        compiler_params=pltpu.CompilerParams(collective_id=1, has_side_effects=True),
    )(x, facts)
    return everything.reshape(-1, everything.shape[2]), facts_all


def halve(parts, axis_name, bit, axis):
    ranks = lax.axis_size(axis_name)
    mine = (lax.axis_index(axis_name) >> bit) & 1
    first, second = [lax.index_in_dim(parts, i, axis, keepdims=False) for i in (0, 1)]
    kept = jnp.where(mine == 0, first, second)
    sent = jnp.where(mine == 0, second, first)
    got = lax.ppermute(sent, axis_name, [(i, i ^ (1 << bit)) for i in range(ranks)])
    return kept.astype(jnp.float32) + got.astype(jnp.float32)


def advance(chunks, number, orders, step):
    states, order = chunks[number], orders[number % 2]
    if len(states) == step + 1:
        axis = sorted(order[step:], reverse=True).index(order[step])
        states.append(halve(states[-1], "dp", order[step], axis).astype(jnp.bfloat16))
    return states[step + 1]


def on_device(hidden, head_weight, critic_in, critic_out, rewards, turn_ids, owners, actions):
    ranks_dp = lax.axis_size("dp")
    ranks_vocab = lax.axis_size("vocab")
    my_dp, my_vocab = lax.axis_index("dp"), lax.axis_index("vocab")
    tok_dev = hidden.shape[0]
    tokens = tok_dev * ranks_dp
    width = hidden.shape[1]
    turn_dev = rewards.shape[1]
    turns = turn_dev * ranks_dp
    slot_count = max(2, 2 * turn_dev // ranks_dp)
    vocab_local = head_weight.shape[1]

    lanes = -(-max(tok_dev, turn_dev) // 128) * 128

    def row(values):
        return jnp.pad(values.astype(jnp.float32), (0, lanes - values.shape[0]))[None, :]

    facts = jnp.concatenate(
        [row(turn_ids[0]), row(owners[:, 0]), row(rewards[0]), jnp.zeros((5, lanes), jnp.float32)]
    )
    hidden_all, facts = gather(hidden, facts)
    ids_all = facts[:, 0, :tok_dev].astype(jnp.int32)
    owner_all = facts[:, 1, :turn_dev].astype(jnp.int32)
    rewards_all = facts[:, 2, :turn_dev]

    position = jnp.arange(tok_dev, dtype=jnp.int32)
    turn_range = jnp.arange(turn_dev, dtype=jnp.int32)
    member = ids_all[:, None, :] == turn_range[None, :, None]
    last_pos = jnp.max(jnp.where(member, position, -1), axis=2)
    earlier = (owner_all[:, None, :] == owner_all[:, :, None]) & (
        turn_range[None, :] < turn_range[:, None]
    )
    slot_of = jnp.sum(earlier.astype(jnp.int32), axis=2)
    per_critic = ranks_dp * slot_count
    place = (owner_all * ranks_dp + jnp.arange(ranks_dp, dtype=jnp.int32)[:, None]) * slot_count
    place = (place + slot_of).reshape(turns)
    end_token = (jnp.arange(ranks_dp, dtype=jnp.int32)[:, None] * tok_dev + last_pos).reshape(turns)
    slots = my_dp * per_critic + jnp.arange(per_critic, dtype=jnp.int32)
    token_of_slot = jnp.sum(
        jnp.where(place[None, :] == slots[:, None], end_token[None, :] + 1, 0), axis=1
    ) - 1
    pick = (jnp.arange(tokens, dtype=jnp.int32)[None, :] == token_of_slot[:, None]).astype(
        jnp.bfloat16
    )
    place_tok = jnp.sum(
        jnp.where(member, place.reshape(ranks_dp, turn_dev)[:, :, None], 0), axis=1
    ).reshape(tokens)
    reward_tok = jnp.sum(jnp.where(member, rewards_all[:, :, None], 0.0), axis=1).reshape(tokens)
    place_own = lax.dynamic_slice_in_dim(place, my_dp * turn_dev, turn_dev, 0)

    rows = jnp.dot(pick, hidden_all, preferred_element_type=jnp.float32)
    normed = rms_norm(rows).astype(jnp.bfloat16)
    inner = jnp.dot(normed, critic_in[0], preferred_element_type=jnp.float32)
    active = jax.nn.silu(inner).astype(jnp.bfloat16)
    value_part = jnp.sum(
        active.astype(jnp.float32) * critic_out[0].astype(jnp.float32)[None, :], axis=1
    )

    logits = jnp.dot(hidden_all, head_weight, preferred_element_type=jnp.float32)
    first_col = (my_dp * ranks_vocab + my_vocab) * vocab_local
    hit = jnp.arange(vocab_local, dtype=jnp.int32)[None, :] == (actions - first_col)[:, None]
    picked_part = jnp.sum(jnp.where(hit, logits, 0.0), axis=1)
    top_part = jnp.max(logits, axis=1)
    mass_part = jnp.sum(jnp.exp(logits - top_part[:, None]), axis=1)

    stats = jnp.stack(
        [top_part, mass_part, picked_part, jnp.pad(value_part, (0, tokens - per_critic))]
        + [jnp.zeros((tokens,), jnp.float32)] * 4
    )
    stats = exchange(stats, 2)
    row_top = jnp.max(stats[:, 0], axis=0)
    row_mass = jnp.sum(stats[:, 1] * jnp.exp(stats[:, 0] - row_top[None, :]), axis=0)
    picked = jnp.sum(stats[:, 2], axis=0)
    logprob_all = picked - row_top - jnp.log(row_mass)
    token_logprob = lax.dynamic_slice_in_dim(logprob_all, my_dp * tok_dev, tok_dev, 0)
    values = jnp.sum(
        stats[:, 3, :per_critic].reshape(ranks_dp, ranks_vocab, per_critic), axis=1
    ).reshape(-1)
    all_places = jnp.arange(ranks_dp * per_critic, dtype=jnp.int32)

    def value_at(places):
        return jnp.sum(jnp.where(places[:, None] == all_places[None, :], values[None, :], 0.0), axis=1)

    advantage = rewards[0] - value_at(place_own)
    token_adv = reward_tok - value_at(place_tok)

    probs = jnp.exp(logits - row_top[:, None]) / row_mass[:, None]
    grad_logits = (loss_scale * token_adv[:, None] * (probs - hit.astype(jnp.float32))).astype(
        jnp.bfloat16
    )
    grad_logits = lax.optimization_barrier(grad_logits)

    dp_bits = list(range(ranks_dp.bit_length() - 1))
    orders = (dp_bits, dp_bits[:1] + dp_bits[:0:-1])
    half = width // 2
    chunks = []
    for number in range(2 * ranks_vocab):
        weight = lax.slice_in_dim(head_weight, number * half, (number + 1) * half, axis=0)
        part = lax.dot_general(
            grad_logits, weight, (((1,), (1,)), ((), ())), preferred_element_type=jnp.float32
        ).astype(jnp.bfloat16)
        chunks.append([part.reshape((2,) * len(dp_bits) + (tok_dev, half))])
    for step in range(len(dp_bits)):
        for number in range(2 * ranks_vocab):
            advance(chunks, number, orders, step)
    blocks = [[chunks[2 * i + k][-1] for k in (0, 1)] for i in range(ranks_vocab)]
    bit = 0
    while len(blocks) > 1:
        joined = []
        for i in range(0, len(blocks), 2):
            pair = []
            for k in (0, 1):
                both = jnp.stack([blocks[i][k], blocks[i + 1][k]])
                pair.append(halve(both, "vocab", bit, 0))
            joined.append(pair)
        blocks = joined
        if len(blocks) > 1:
            blocks = [[x.astype(jnp.bfloat16) for x in pair] for pair in blocks]
        bit += 1
    hidden_grad = jnp.concatenate(blocks[0], axis=1)
    return (hidden_grad, token_logprob, advantage[None, :])


def solution(mesh):
    return jax.shard_map(
        on_device,
        mesh=mesh,
        in_specs=(
            P("dp", "vocab"),
            P(None, ("dp", "vocab")),
            P("dp", None, "vocab"),
            P("dp", "vocab"),
            P("dp", None),
            P("dp", None),
            P("dp", None),
            P(),
        ),
        out_specs=(P("dp", "vocab"), P("dp"), P("dp", None)),
        check_vma=False,
    )
```
